32 devices in a mesh: section: 2 (over core), expert: 8 (over z, x), dp: 2 (over y).
Axes of the slice: x: 2, y: 2, z: 4, core: 2. Of those that a mesh axis runs over, the one named last changes fastest.
Arguments:
- tokens: bfloat16 [4, 512, 2048], P(None, ('expert', 'dp')), may hold values from -6 to 6
- routes: int32 [2, 4, 512, 2], P('section', None, ('expert', 'dp')), may hold values from 0 to 7, all different within a row; in each aligned block of 32 rows (0 to 31, 32 to 63, ..., all dimensions but the last counted through in order) at most 9 rows name the same one
- gate_probs: float32 [2, 4, 512, 2], P('section', None, ('expert', 'dp')), may hold values from 0.1 to 1
- w_gate: bfloat16 [2, 8, 2048, 640], P('section', 'expert'), may hold values from -0.125 to 0.125
- w_up: bfloat16 [2, 8, 2048, 640], P('section', 'expert'), may hold values from -0.125 to 0.125
- w_down: bfloat16 [2, 8, 640, 2048], P('section', 'expert'), may hold values from -0.25 to 0.25
- cotangent: bfloat16 [4, 512, 2048], P(None, ('expert', 'dp')), may hold values from -0.29882812 to 0.29882812
Outputs:
- grad_gate: float32 [2, 8, 2048, 640], P('section', 'expert', 'dp')
- grad_up: float32 [2, 8, 2048, 640], P('section', 'expert', 'dp')
- grad_down: float32 [2, 8, 640, 2048], P('section', 'expert', None, 'dp')
The draws below stay inside these ranges and needn't reach their ends.
Inputs may be any that keep to these rules, and one draw needn't show every extreme that they name: `routes`: in each micro-batch and layer, the 32 token rows of one device (aligned blocks) name each expert at most 9 times, a bound that some block reaches; the 2 experts of a token differ.
All inputs are finite; a program needn't handle non-finite values.
Results may differ from the reference program's by a relative error of at most 0.015.
Values may be sent and summed in bfloat16 or wider, within the bound.
No kernel may reach another device: no remote copies, remote signals or barrier semaphores. Data moves between devices by JAX's collectives and lax.ppermute only.
A program may use at most 64 MiB of HBM per device.

```python
import math
import jax
import jax.numpy as jnp
import numpy as np
from jax import lax

D = 2048
FF_DEV = 640
TOP = 2
M = 4
ROWS = 32
EXPERTS = 8
CAP = 9
TOKENS = 512
N_SECTION = 2
N_EXPERT = 8
N_DP = 2


def steps_of(stream_key, dims, pieces, least, high):
    loudness = 1.0
    for dim, blocks in pieces:
        heights = jax.random.uniform(jax.random.fold_in(jax.random.fold_in(stream_key, 6), dim), (blocks,), jnp.float32, least / len(pieces), high / len(pieces))
        loudness = loudness * jnp.repeat(jnp.exp(heights), dims[dim] // blocks).reshape((-1,) + (1,) * (len(dims) - 1 - dim))
    return loudness


def deal_out(own_key, own, number, rows, number_of, top, reach, slope):
    sequence = jax.random.permutation(own_key, number_of)
    packed, usual = portions_of(number_of, rows * top, reach, slope, True), portions_of(number_of, rows * top, reach, slope, False)
    places = jnp.arange(number_of)

    def named(lengths, rotation):
        used = int((lengths > 0).sum())
        fixed = max(1, used // 4)
        moved = fixed + (places - fixed + rotation * (used - fixed)) % max(1, number_of - fixed)
        return jnp.zeros((number_of,), jnp.int32).at[sequence[jnp.where(places < fixed, places, moved)]].set(jnp.asarray(lengths, jnp.int32))

    lengths = jnp.where(number % 4 == 0, named(packed, number // 4), named(usual, number - number // 4 - 1))
    mixed = jax.random.permutation(jax.random.fold_in(own, 3), number_of)
    source_of, sink = mixed[0:number_of // 2 * 2:2], mixed[1:number_of // 2 * 2:2]
    slack = jnp.minimum(lengths[source_of] - 1, reach - lengths[sink]) // 2
    slack = jnp.where((source_of == sequence[0]) | (sink == sequence[0]) | (lengths[sink] == 0), 0, jnp.maximum(slack, 0))
    moved = jax.random.randint(jax.random.fold_in(own, 4), (number_of // 2,), 0, 1 << 20) % (slack + 1)
    lengths = lengths.at[source_of].add(-moved).at[sink].add(moved)
    members = jnp.searchsorted(jnp.cumsum(lengths), jnp.arange(rows * top), side="right").astype(jnp.int32)
    table = members.reshape(top, rows).T
    table = table[jax.random.permutation(jax.random.fold_in(own, 1), rows)]
    rotation = jax.random.randint(jax.random.fold_in(own, 2), (rows, 1), 0, top)
    return jnp.take_along_axis(table, (jnp.arange(top)[None, :] + rotation) % top, axis=1)


def portions_of(number_of, total, most, slope, full):
    loads = [(1 << 20) // math.isqrt(rank ** slope) + 1 for rank in range(1, number_of + 1)]
    largest = most if full else min(most, max(-(-total // number_of), total * loads[0] // sum(loads)))
    least = 1 if total - largest >= number_of - 1 else 0
    holding, spare = [largest] + [least] * (number_of - 1), total - largest - least * (number_of - 1)
    while spare > 0:
        movable = [i for i in range(1, number_of) if holding[i] < largest] or [i for i in range(1, number_of) if holding[i] < most]
        mass, left = sum([loads[i] for i in movable]), spare
        for i in movable:
            addition = min(most - holding[i], max(1, left * loads[i] // mass), spare)
            holding[i] = holding[i] + addition
            spare = spare - addition
    return np.array(holding)


def centred(stream_key, dims, deviation, reach, cuts=(), held_as=jnp.bfloat16):
    gain = steps_of(stream_key, dims, cuts, -0.22, 0.18) if cuts else 1.0
    result = jax.random.normal(stream_key, dims, jnp.float32) * deviation * gain
    return jnp.minimum(jnp.maximum(result, -reach), reach).astype(held_as)


def setup_inputs(seed: int = 0) -> dict:
    arg_keys = jax.random.split(jax.random.key(seed), 8)
    tokens = centred(arg_keys[0], (M, TOKENS, D), 1.0, 6.0, ((1, 16),))
    routes_keys = jax.random.split(jax.random.fold_in(arg_keys[1], 1), N_SECTION * M * TOKENS // ROWS)
    routes_turns = jax.random.permutation(jax.random.fold_in(arg_keys[1], 3), N_SECTION * M * TOKENS // ROWS)
    routes = jax.vmap(lambda own, number: deal_out(jax.random.fold_in(arg_keys[1], 2), own, number, ROWS, EXPERTS, TOP, CAP, 2))(routes_keys, routes_turns).reshape((N_SECTION, M, TOKENS, TOP))
    gate_probs = jnp.clip(jnp.exp(math.log(1.0) - 2.3025851 * jax.random.uniform(arg_keys[2], (N_SECTION, M, TOKENS, TOP), jnp.float32) ** steps_of(arg_keys[2], (N_SECTION, M, TOKENS, TOP), ((0, 2), (2, 16)), -0.2, 0.2)), 0.1, 1.0)
    w_gate = centred(arg_keys[3], (N_SECTION, EXPERTS, D, FF_DEV), D ** -0.5, 0.125, ((0, 2), (1, 8)))
    w_up = centred(arg_keys[4], (N_SECTION, EXPERTS, D, FF_DEV), D ** -0.5, 0.125, ((0, 2), (1, 8)))
    w_down = centred(arg_keys[5], (N_SECTION, EXPERTS, FF_DEV, D), FF_DEV ** -0.5, 0.25, ((0, 2), (1, 8)))
    cotangent = centred(arg_keys[6], (M, TOKENS, D), 0.05, 0.29882812, ((1, 16),))
    return {"tokens": tokens, "routes": routes, "gate_probs": gate_probs, "w_gate": w_gate, "w_up": w_up, "w_down": w_down, "cotangent": cotangent}


epsilon = 1e-05

def inverse_rms(values):
    return lax.rsqrt(lax.optimization_barrier(jnp.mean(values * values, -1, keepdims=True)) + epsilon)

def route_slots(route_ids):
    flat_ids = route_ids.reshape(-1).astype(jnp.int32)
    one_hot = (flat_ids[:, None] == jnp.arange(EXPERTS, dtype=jnp.int32)[None, :]).astype(jnp.int32)
    earlier = jnp.cumsum(one_hot, 0) - one_hot
    slot_num = lax.optimization_barrier(jnp.sum(earlier * one_hot, 1)).astype(jnp.int32)
    return (flat_ids, slot_num)

def expert_inputs(normed, flat_ids, slot_num):
    buffer_rows = N_EXPERT * N_DP * CAP
    token_of_pair = (jnp.arange(TOKENS * TOP, dtype=jnp.int32) // TOP).astype(jnp.int32)
    table = jnp.full((EXPERTS, buffer_rows), TOKENS, dtype=jnp.int32).at[flat_ids, slot_num].set(token_of_pair)
    padded = jnp.concatenate([normed, jnp.zeros((1, D), normed.dtype)], 0)
    return padded[table]

def pre_activations(rows_in, gate_mats, up_mats):
    rows_f = rows_in.astype(jnp.float32)
    pre_gate = jnp.einsum('ebd,edf->ebf', rows_f, gate_mats.astype(jnp.float32))
    pre_up = jnp.einsum('ebd,edf->ebf', rows_f, up_mats.astype(jnp.float32))
    return (pre_gate, pre_up)

def layer_forward(current, route_ids, probs, gate_mats, up_mats, down_mats):
    current_f = current.astype(jnp.float32)
    normed = (current_f * inverse_rms(current_f)).astype(jnp.bfloat16)
    flat_ids, slot_num = route_slots(route_ids)
    rows_in = expert_inputs(normed, flat_ids, slot_num)
    pre_gate, pre_up = pre_activations(rows_in, gate_mats, up_mats)
    activation = (jax.nn.silu(pre_gate) * pre_up).astype(jnp.bfloat16)
    produced = jnp.einsum('ebf,efd->ebd', activation.astype(jnp.float32), down_mats.astype(jnp.float32)).astype(jnp.bfloat16)
    chosen = produced[flat_ids, slot_num].reshape(TOKENS, TOP, D).astype(jnp.float32)
    return (current_f + lax.optimization_barrier(jnp.sum(probs[:, :, None] * chosen, 1))).astype(jnp.bfloat16)

def layer_backward(current, upstream, route_ids, probs, gate_mats, up_mats, down_mats):
    buffer_rows = N_EXPERT * N_DP * CAP
    current_f = current.astype(jnp.float32)
    scale_rms = inverse_rms(current_f)
    normed = (current_f * scale_rms).astype(jnp.bfloat16)
    flat_ids, slot_num = route_slots(route_ids)
    rows_in = expert_inputs(normed, flat_ids, slot_num)
    pre_gate, pre_up = pre_activations(rows_in, gate_mats, up_mats)
    upstream_f = upstream.astype(jnp.float32)
    scaled = (probs[:, :, None] * upstream_f[:, None, :]).astype(jnp.bfloat16).reshape(TOKENS * TOP, D)
    arrived = jnp.zeros((EXPERTS, buffer_rows, D), jnp.bfloat16).at[flat_ids, slot_num].set(scaled)
    back_hidden = jnp.einsum('ebd,efd->ebf', arrived.astype(jnp.float32), down_mats.astype(jnp.float32))
    sigmoid_gate = jax.nn.sigmoid(pre_gate)
    silu_gate = pre_gate * sigmoid_gate
    d_gate = (back_hidden * pre_up * sigmoid_gate * (1.0 + pre_gate * (1.0 - sigmoid_gate))).astype(jnp.bfloat16)
    d_up = (back_hidden * silu_gate).astype(jnp.bfloat16)
    activation = (silu_gate * pre_up).astype(jnp.bfloat16)
    d_rows = (jnp.einsum('ebf,edf->ebd', d_gate.astype(jnp.float32), gate_mats.astype(jnp.float32)) + jnp.einsum('ebf,edf->ebd', d_up.astype(jnp.float32), up_mats.astype(jnp.float32))).astype(jnp.bfloat16)
    rows_f = rows_in.astype(jnp.float32)
    part_gate = jnp.einsum('ebd,ebf->edf', rows_f, d_gate.astype(jnp.float32))
    part_up = jnp.einsum('ebd,ebf->edf', rows_f, d_up.astype(jnp.float32))
    part_down = jnp.einsum('ebf,ebd->efd', activation.astype(jnp.float32), arrived.astype(jnp.float32))
    d_normed = lax.optimization_barrier(jnp.sum(d_rows[flat_ids, slot_num].reshape(TOKENS, TOP, D).astype(jnp.float32), 1))
    d_current = scale_rms * d_normed - current_f * scale_rms ** 3 * lax.optimization_barrier(jnp.mean(d_normed * current_f, -1, keepdims=True))
    passed = (upstream_f + d_current).astype(jnp.bfloat16)
    return (passed, part_gate, part_up, part_down)

def reference(tokens, routes, gate_probs, w_gate, w_up, w_down, cotangent):
    saved = []
    layer_acts = [tokens[micro_num] for micro_num in range(M)]
    for section_num in range(N_SECTION):
        saved.append(layer_acts)
        layer_acts = [layer_forward(layer_acts[micro_num], routes[section_num, micro_num], gate_probs[section_num, micro_num], w_gate[section_num], w_up[section_num], w_down[section_num]) for micro_num in range(M)]
    upstream = [cotangent[micro_num] for micro_num in range(M)]
    grads_gate = [None] * N_SECTION
    grads_up = [None] * N_SECTION
    grads_down = [None] * N_SECTION
    for section_num in reversed(range(N_SECTION)):
        total_gate = jnp.zeros((EXPERTS, D, FF_DEV), jnp.float32)
        total_up = jnp.zeros((EXPERTS, D, FF_DEV), jnp.float32)
        total_down = jnp.zeros((EXPERTS, FF_DEV, D), jnp.float32)
        next_upstream = []
        for micro_num in range(M):
            passed, part_gate, part_up, part_down = layer_backward(saved[section_num][micro_num], upstream[micro_num], routes[section_num, micro_num], gate_probs[section_num, micro_num], w_gate[section_num], w_up[section_num], w_down[section_num])
            total_gate = total_gate + part_gate
            total_up = total_up + part_up
            total_down = total_down + part_down
            next_upstream.append(passed)
        upstream = next_upstream
        grads_gate[section_num] = total_gate
        grads_up[section_num] = total_up
        grads_down[section_num] = total_down
    return (jnp.stack(grads_gate), jnp.stack(grads_up), jnp.stack(grads_down))
```

```python
import jax
import jax.numpy as jnp
import numpy as np
from jax import lax
from jax.experimental import pallas as pl
from jax.experimental.pallas import tpu as pltpu
from jax.sharding import PartitionSpec as P


epsilon = 1e-05
bf16 = jnp.bfloat16
f32 = jnp.float32
nt_dims = (((1,), (1,)), ((), ()))
tn_dims = (((0,), (0,)), ((), ()))
ANY = pl.BlockSpec(memory_space=pl.ANY)
VMEM = pl.BlockSpec(memory_space=pltpu.VMEM)
SMEM = pl.BlockSpec(memory_space=pltpu.SMEM)


def dot(a, b):
    return jnp.dot(a, b, preferred_element_type=f32)


def dot_nt(a, b):
    return lax.dot_general(a, b, nt_dims, preferred_element_type=f32)


def dot_tn(a, b):
    return lax.dot_general(a, b, tn_dims, preferred_element_type=f32)


class Sizes:
    def __init__(self, tokens, routes, w_gate):
        micro, rows, self.width = tokens.shape
        self.experts = lax.axis_size("expert")
        self.sections = lax.axis_size("section")
        self.dp = lax.axis_size("dp")
        top = routes.shape[-1]
        self.top = top
        self.hidden = w_gate.shape[-1]
        groups = micro // self.sections
        self.groups = groups
        self.tok = groups * rows
        self.cap = groups * min(rows, rows * top // self.experts + 1)
        pieces = 1
        while self.cap * pieces % 8:
            pieces *= 2
        self.pieces = pieces
        self.pw = self.width // pieces
        self.main = self.cap // 16 * 16
        self.rest = self.cap - self.main
        self.chunk = self.cap * pieces
        self.slots = self.experts * self.cap
        self.part = self.width // self.dp


def rest_mixer(z):
    per = z.experts * z.rest
    mat = np.zeros((z.pieces * per, z.experts * z.pieces * z.rest), np.float32)
    for c in range(z.experts):
        for p in range(z.pieces):
            for r in range(z.rest):
                mat[p * per + c * z.rest + r, c * z.pieces * z.rest + p * z.rest + r] = 1
    return jnp.asarray(mat, bf16)


def to_pieces(z, value):
    return jnp.concatenate([value[:, p * z.pw : (p + 1) * z.pw] for p in range(z.pieces)], 0)


def sum_pieces(z, column):
    total = column[: z.tok]
    for p in range(1, z.pieces):
        total = total + column[p * z.tok : (p + 1) * z.tok]
    return jnp.concatenate([total] * z.pieces, 0)


def gather_rows(z, chunks, mixer, dst):
    for c in range(z.experts):
        for p in range(z.pieces):
            if z.main:
                dst[c * z.main : (c + 1) * z.main, p * z.pw : (p + 1) * z.pw] = chunks[c][
                    p * z.main : (p + 1) * z.main, :
                ]
    base = z.experts * z.main
    per = z.experts * z.rest
    if z.rest:
        tail = jnp.concatenate([chunks[c][z.pieces * z.main :, :] for c in range(z.experts)], 0)
        mixed = dot(mixer[...], tail).astype(bf16)
        for p in range(z.pieces):
            dst[base : base + per, p * z.pw : (p + 1) * z.pw] = mixed[p * per : (p + 1) * per]


def scatter_rows(z, value, mixer, chunks):
    for c in range(z.experts):
        for p in range(z.pieces):
            if z.main:
                chunks[c][p * z.main : (p + 1) * z.main, :] = value[
                    c * z.main : (c + 1) * z.main, p * z.pw : (p + 1) * z.pw
                ]
    base = z.experts * z.main
    per = z.pieces * z.rest
    if z.rest:
        tail = to_pieces(z, value[base:])
        mixed = dot_tn(mixer[...], tail).astype(bf16)
        for c in range(z.experts):
            chunks[c][z.pieces * z.main :, :] = mixed[c * per : (c + 1) * per]


def selector(z, row):
    number = lax.broadcasted_iota(jnp.int32, (z.experts * z.chunk, z.pieces * z.tok), 0)
    return (number.astype(f32) == row).astype(bf16)


def selector_t(z, column):
    number = lax.broadcasted_iota(jnp.int32, (z.pieces * z.tok, z.experts * z.chunk), 1)
    return (number.astype(f32) == column).astype(bf16)


def write_chunks(z, value, outs):
    for c in range(z.experts):
        outs[c][...] = value[c * z.chunk : (c + 1) * z.chunk]


def read_chunks(z, refs):
    return jnp.concatenate([r[...] for r in refs], 0)


def slot_place(z, ids, pos, piece):
    inside = pos < z.main
    base = ids * z.chunk + jnp.where(inside, pos, z.pieces * z.main + pos - z.main)
    return base + piece * jnp.where(inside, float(z.main), float(z.rest))


def start_kernel(z, sec, mine, theirs, tokens, rowtab, coltab, *outs):
    first = sec[0] == 0
    a, b = mine[...], theirs[...]
    layers = (jnp.where(first, a, b), jnp.where(first, b, a))
    wide = z.pieces * z.tok
    row_t = lax.broadcasted_iota(jnp.int32, (z.tok, wide), 0)
    lane = lax.broadcasted_iota(jnp.int32, (1, wide), 1)
    lane_p = jnp.zeros((1, wide), jnp.int32)
    for p in range(1, z.pieces):
        lane_p = lane_p + (lane >= p * z.tok).astype(jnp.int32)
    lane_t = lane - lane_p * z.tok
    same = row_t == lane_t
    before = row_t < lane_t
    col_t = lax.broadcasted_iota(jnp.int32, (z.tok, z.tok), 0)
    col_u = lax.broadcasted_iota(jnp.int32, (z.tok, z.tok), 1)
    narrow_same = col_t == col_u
    narrow_before = col_u < col_t
    row_list = []
    col_list = []
    for layer in layers:
        cols = [layer[:, k : k + 1] for k in range(z.top)]
        rows = [jnp.sum(jnp.where(same, c, 0.0), 0, keepdims=True) for c in cols]
        thin = [jnp.sum(jnp.where(narrow_same, c, 0.0), 0, keepdims=True) for c in cols]
        for k in range(z.top):
            count = sum((c == rows[k]).astype(f32) for c in cols)
            pos = jnp.sum(jnp.where(before, count, 0.0), 0, keepdims=True)
            row_list.append(slot_place(z, rows[k], pos, lane_p.astype(f32)))
            count = sum((cols[k] == r).astype(f32) for r in thin)
            pos = jnp.sum(jnp.where(narrow_before, count, 0.0), 1, keepdims=True)
            col_list.append(
                jnp.concatenate(
                    [slot_place(z, cols[k], pos, float(p)) for p in range(z.pieces)], 0
                )
            )
    for layer in layers:
        for k in range(z.top):
            col_list.append(
                jnp.concatenate([layer[:, z.top + k : z.top + k + 1]] * z.pieces, 0)
            )
    lanes = lax.broadcasted_iota(jnp.int32, coltab.shape, 1)
    packed = jnp.zeros(coltab.shape, f32)
    for j, col in enumerate(col_list):
        packed = jnp.where(lanes == j, col, packed)
    coltab[...] = packed
    for j, row in enumerate(row_list):
        rowtab[j : j + 1, :] = row
    x = tokens[...].astype(f32)
    inv = lax.rsqrt(jnp.mean(x * x, -1, keepdims=True) + epsilon)
    normed = to_pieces(z, (x * inv).astype(bf16))
    select = sum(selector(z, row_list[k]) for k in range(z.top))
    write_chunks(z, dot(select, normed).astype(bf16), outs)


def scaled_dispatch(z, upstream, rowtab, coltab, layer, outs):
    total = 0.0
    probs = z.sections * z.top
    for k in range(z.top):
        at = layer * z.top + k
        scaled = (coltab[:, probs + at : probs + at + 1] * upstream).astype(bf16)
        total = total + dot(selector(z, rowtab[at : at + 1, :]), scaled)
    write_chunks(z, total.astype(bf16), outs)


def cotangent_kernel(z, rowtab, coltab, cot, *outs):
    scaled_dispatch(z, to_pieces(z, cot[...]).astype(f32), rowtab, coltab, 1, outs)


def load_start(sec, layer, own, other, dst, sem):
    mine = sec[0] == layer

    @pl.when(mine)
    def _():
        pltpu.make_async_copy(own, dst, sem).start()

    @pl.when(jnp.logical_not(mine))
    def _():
        pltpu.make_async_copy(other, dst, sem).start()


def load_wait(own, dst, sem):
    pltpu.make_async_copy(own, dst, sem).wait()


def write_parts(z, dp_pos, src, outs):
    for m in range(z.dp):

        @pl.when(dp_pos == m)
        def _():
            for k in range(z.dp):
                at = (m ^ k) * z.part
                outs[k][...] = src[:, at : at + z.part]


def forward_kernel(z, sec, mixer, *refs):
    recv = refs[: z.experts]
    weights = refs[z.experts : z.experts + 6]
    outs = refs[z.experts + 6 : 2 * z.experts + 6]
    rest = refs[2 * z.experts + 6 :]
    parts = rest[: z.dp]
    act_out, gate_out, up_out, rows, vg, vu, vd, sems = rest[z.dp :]
    scratch = (vg, vu, vd)
    for i in range(3):
        load_start(sec, 0, weights[2 * i], weights[2 * i + 1], scratch[i], sems.at[i])
    gather_rows(z, recv, mixer, rows)
    write_parts(z, sec[1], rows, parts)
    load_wait(weights[0], vg, sems.at[0])
    gate = dot(rows[...], vg[...])
    load_wait(weights[2], vu, sems.at[1])
    up = dot(rows[...], vu[...])
    gate_out[...] = gate
    up_out[...] = up
    act = (gate * jax.nn.sigmoid(gate) * up).astype(bf16)
    act_out[...] = act
    load_wait(weights[4], vd, sems.at[2])
    scatter_rows(z, dot(act, vd[...]).astype(bf16), mixer, outs)


def middle_kernel(z, rowtab, coltab, tokens, *refs):
    recv = refs[: z.experts]
    kept = refs[z.experts]
    outs = refs[z.experts + 1 :]
    back = read_chunks(z, recv)
    probs = z.sections * z.top
    mixed = 0.0
    for k in range(z.top):
        chosen = dot(selector_t(z, coltab[:, k : k + 1]), back)
        mixed = mixed + coltab[:, probs + k : probs + k + 1] * chosen
    x = (to_pieces(z, tokens[...]).astype(f32) + mixed).astype(bf16)
    kept[...] = x
    xf = x.astype(f32)
    square = sum_pieces(z, jnp.sum(xf * xf, -1, keepdims=True))
    normed = (xf * lax.rsqrt(square / z.width + epsilon)).astype(bf16)
    select = sum(selector(z, rowtab[z.top + k : z.top + k + 1, :]) for k in range(z.top))
    write_chunks(z, dot(select, normed).astype(bf16), outs)


def hidden_grads(gate, up, back):
    sg = jax.nn.sigmoid(gate)
    silu = gate * sg
    d_gate = (back * up * sg * (1.0 + gate * (1.0 - sg))).astype(bf16)
    d_up = (back * silu).astype(bf16)
    return d_gate, d_up, (silu * up).astype(bf16)


def turn_kernel(z, sec, mixer, *refs):
    n = z.experts
    recv, given = refs[:n], refs[n : 2 * n]
    weights = refs[2 * n : 2 * n + 6]
    outs = refs[2 * n + 6 : 3 * n + 6]
    rest = refs[3 * n + 6 :]
    row_parts, go_parts = rest[: z.dp], rest[z.dp : 2 * z.dp]
    act_out, dgu_out, rows, go, vg, vu, vd, sems = rest[2 * z.dp :]
    scratch = (vg, vu, vd)
    for i in range(3):
        load_start(sec, 1, weights[2 * i], weights[2 * i + 1], scratch[i], sems.at[i])
    gather_rows(z, recv, mixer, rows)
    gather_rows(z, given, mixer, go)
    load_wait(weights[0], vg, sems.at[0])
    gate = dot(rows[...], vg[...])
    load_wait(weights[2], vu, sems.at[1])
    up = dot(rows[...], vu[...])
    load_wait(weights[4], vd, sems.at[2])
    back = dot_nt(go[...], vd[...])
    d_gate, d_up, act = hidden_grads(gate, up, back)
    act_out[...] = act
    dgu_out[:, : z.hidden] = d_gate
    dgu_out[:, z.hidden :] = d_up
    d_rows = (dot_nt(d_gate, vg[...]) + dot_nt(d_up, vu[...])).astype(bf16)
    scatter_rows(z, d_rows, mixer, outs)
    write_parts(z, sec[1], rows, row_parts)
    write_parts(z, sec[1], go, go_parts)


def upstream_kernel(z, rowtab, coltab, kept, cot, *refs):
    recv = refs[: z.experts]
    outs = refs[z.experts :]
    back = read_chunks(z, recv)
    select = sum(
        selector_t(z, coltab[:, z.top + k : z.top + k + 1]) for k in range(z.top)
    )
    d_normed = dot(select, back)
    xf = kept[...].astype(f32)
    square = sum_pieces(z, jnp.sum(xf * xf, -1, keepdims=True))
    inv = lax.rsqrt(square / z.width + epsilon)
    inner = sum_pieces(z, jnp.sum(d_normed * xf, -1, keepdims=True)) / z.width
    d_x = inv * d_normed - xf * (inv * inv * inv) * inner
    upstream = (to_pieces(z, cot[...]).astype(f32) + d_x).astype(bf16).astype(f32)
    scaled_dispatch(z, upstream, rowtab, coltab, 0, outs)


def backward_kernel(z, sec, mixer, gate, up, *refs):
    recv = refs[: z.experts]
    own, other = refs[z.experts : z.experts + 2]
    rest = refs[z.experts + 2 :]
    parts = rest[: z.dp]
    dgu_out, go, vd, sems = rest[z.dp :]
    load_start(sec, 0, own, other, vd, sems.at[0])
    gather_rows(z, recv, mixer, go)
    write_parts(z, sec[1], go, parts)
    load_wait(own, vd, sems.at[0])
    back = dot_nt(go[...], vd[...])
    d_gate, d_up, _ = hidden_grads(gate[...], up[...], back)
    dgu_out[:, : z.hidden] = d_gate
    dgu_out[:, z.hidden :] = d_up


def grads_kernel(z, count, sec, *refs):
    sets = (refs[: 4 * count], refs[4 * count : 8 * count])
    out_gate, out_up, out_down = refs[8 * count : 8 * count + 3]
    scratch = refs[8 * count + 3 : 8 * count + 7]
    buf_gate, buf_up, buf_down, sems, out_sems = refs[8 * count + 7 :]
    for layer in range(2):

        @pl.when(sec[0] == layer)
        def _():
            for kind in range(4):
                for g in range(count):
                    pltpu.make_async_copy(
                        sets[layer][kind * count + g],
                        scratch[kind].at[pl.ds(g * z.slots, z.slots)],
                        sems.at[kind],
                    ).start()

    def wait(kind):
        for g in range(count):
            pltpu.make_async_copy(
                sets[0][kind * count + g],
                scratch[kind].at[pl.ds(g * z.slots, z.slots)],
                sems.at[kind],
            ).wait()

    rows, act, go, dgu = scratch
    wait(0)
    wait(3)
    buf_gate[...] = dot_tn(rows[...], dgu[:, : z.hidden])
    copy_gate = pltpu.make_async_copy(buf_gate, out_gate, out_sems.at[0])
    copy_gate.start()
    buf_up[...] = dot_tn(rows[...], dgu[:, z.hidden :])
    copy_up = pltpu.make_async_copy(buf_up, out_up, out_sems.at[1])
    copy_up.start()
    wait(1)
    wait(2)
    buf_down[...] = dot_tn(act[...], go[...])
    copy_down = pltpu.make_async_copy(buf_down, out_down, out_sems.at[2])
    copy_down.start()
    copy_gate.wait()
    copy_up.wait()
    copy_down.wait()


def exchange(axis, parts):
    size = lax.axis_size(axis)
    out = [parts[0]]
    for k in range(1, size):
        out.append(lax.ppermute(parts[k], axis, [(i, i ^ k) for i in range(size)]))
    return out


def shards(tokens, routes, gate_probs, w_gate, w_up, w_down, cotangent):
    z = Sizes(tokens, routes, w_gate)
    sec_pos = lax.axis_index("section")
    expert_pos = lax.axis_index("expert")
    dp_pos = lax.axis_index("dp")
    sec = jnp.stack([sec_pos, dp_pos]).astype(jnp.int32)
    weights = (w_gate[0, 0], w_up[0, 0], w_down[0, 0])

    def swap(value):
        return lax.ppermute(value, "section", [(0, 1), (1, 0)])

    relative = (routes[0] ^ expert_pos).astype(f32)
    packed = jnp.concatenate([relative, gate_probs[0]], -1)
    packed = packed.reshape(z.sections, z.tok, 2 * z.top)
    mine = lax.dynamic_index_in_dim(packed, sec_pos, 0, keepdims=False)
    theirs = swap(lax.dynamic_index_in_dim(packed, 1 - sec_pos, 0, keepdims=False))
    others = tuple(swap(w) for w in weights)
    pairs = [w for own, other in zip(weights, others) for w in (own, other)]

    def half(value):
        value = value.reshape(z.sections, z.tok, z.width)
        return lax.dynamic_index_in_dim(value, sec_pos, 0, keepdims=False)

    x0 = half(tokens)
    cot = half(cotangent)
    mixer = rest_mixer(z)
    chunk = jax.ShapeDtypeStruct((z.chunk, z.pw), bf16)
    chunks = [chunk] * z.experts
    part = jax.ShapeDtypeStruct((z.slots, z.part), bf16)
    hid = lambda n, t: jax.ShapeDtypeStruct((z.slots, n * z.hidden), t)
    rowtab_s = jax.ShapeDtypeStruct((8, z.pieces * z.tok), f32)
    coltab_s = jax.ShapeDtypeStruct((z.pieces * z.tok, 8), f32)
    vm = lambda *s: pltpu.VMEM(s, bf16)
    row_buf = vm(z.slots, z.width)
    wide_w = vm(z.width, z.hidden)
    down_w = vm(z.hidden, z.width)

    def call(body, name, ins, outs, scratch=()):
        return pl.pallas_call(
            lambda *refs: body(z, *refs),
            in_specs=ins,
            out_shape=outs,
            out_specs=[VMEM] * len(outs),
            scratch_shapes=list(scratch),
            name=name,
        )

    ne = z.experts
    rowtab, coltab, *send = call(
        start_kernel, "start", [SMEM, VMEM, VMEM, VMEM], [rowtab_s, coltab_s] + chunks
    )(sec, mine, theirs, x0)
    recv = exchange("expert", send)
    send_c = call(cotangent_kernel, "cotangent", [VMEM] * 3, chunks)(rowtab, coltab, cot)
    given = exchange("expert", send_c)

    out = call(
        forward_kernel,
        "forward",
        [SMEM, VMEM] + [VMEM] * ne + [ANY] * 6,
        chunks + [part] * z.dp + [hid(1, bf16), hid(1, f32), hid(1, f32)],
        [row_buf, wide_w, wide_w, down_w, pltpu.SemaphoreType.DMA((3,))],
    )(sec, mixer, *recv, *pairs)
    send, row_parts0 = out[:ne], out[ne : ne + z.dp]
    act0, gate0, up0 = out[ne + z.dp :]
    recv = exchange("expert", send)
    kept, *send = call(
        middle_kernel,
        "middle",
        [VMEM] * (3 + ne),
        [jax.ShapeDtypeStruct((z.pieces * z.tok, z.pw), bf16)] + chunks,
    )(rowtab, coltab, x0, *recv)
    recv = exchange("expert", send)
    out = call(
        turn_kernel,
        "turn",
        [SMEM, VMEM] + [VMEM] * (2 * ne) + [ANY] * 6,
        chunks + [part] * (2 * z.dp) + [hid(1, bf16), hid(2, bf16)],
        [row_buf, row_buf, wide_w, wide_w, down_w, pltpu.SemaphoreType.DMA((3,))],
    )(sec, mixer, *recv, *given, *pairs)
    send = out[:ne]
    row_parts1, go_parts1 = out[ne : ne + z.dp], out[ne + z.dp : ne + 2 * z.dp]
    act1, dgu1 = out[ne + 2 * z.dp :]
    recv = exchange("expert", send)
    send = call(upstream_kernel, "upstream", [VMEM] * (4 + ne), chunks)(
        rowtab, coltab, kept, cot, *recv
    )
    recv = exchange("expert", send)
    out = call(
        backward_kernel,
        "backward",
        [SMEM, VMEM, VMEM, VMEM] + [VMEM] * ne + [ANY] * 2,
        [part] * z.dp + [hid(2, bf16)],
        [row_buf, down_w, pltpu.SemaphoreType.DMA((1,))],
    )(sec, mixer, gate0, up0, *recv, *pairs[4:])
    go_parts0, dgu0 = out[: z.dp], out[z.dp]

    def spread(parts):
        here = exchange("dp", parts)
        return here + [swap(v) for v in here]

    same = lambda v: [v] * z.dp
    set0 = spread(row_parts0) + spread(same(act0)) + spread(go_parts0) + spread(same(dgu0))
    set1 = spread(row_parts1) + spread(same(act1)) + spread(go_parts1) + spread(same(dgu1))
    count = z.dp * z.sections
    total = count * z.slots
    grad_shapes = [
        jax.ShapeDtypeStruct((z.part, z.hidden), f32),
        jax.ShapeDtypeStruct((z.part, z.hidden), f32),
        jax.ShapeDtypeStruct((z.hidden, z.part), f32),
    ]
    grads = pl.pallas_call(
        lambda *refs: grads_kernel(z, count, *refs),
        in_specs=[SMEM] + [ANY] * (8 * count),
        out_shape=grad_shapes,
        out_specs=[ANY] * 3,
        scratch_shapes=[
            vm(total, z.part),
            vm(total, z.hidden),
            vm(total, z.part),
            vm(total, 2 * z.hidden),
        ]
        + [pltpu.VMEM(s.shape, f32) for s in grad_shapes]
        + [pltpu.SemaphoreType.DMA((4,)), pltpu.SemaphoreType.DMA((3,))],
        name="grads",
    )(sec, *set0, *set1)
    return tuple(g[None, None] for g in grads)


def solution(mesh):
    in_specs = (
        P(None, ("expert", "dp"), None),
        P("section", None, ("expert", "dp"), None),
        P("section", None, ("expert", "dp"), None),
        P("section", "expert", None, None),
        P("section", "expert", None, None),
        P("section", "expert", None, None),
        P(None, ("expert", "dp"), None),
    )
    out_specs = (
        P("section", "expert", "dp", None),
        P("section", "expert", "dp", None),
        P("section", "expert", None, "dp"),
    )
    return jax.shard_map(shards, mesh=mesh, in_specs=in_specs, out_specs=out_specs, check_vma=False)
```

```python
import jax
import jax.numpy as jnp
import numpy as np
from jax import lax
from jax.experimental import pallas as pl
from jax.experimental.pallas import tpu as pltpu
from jax.sharding import PartitionSpec as P


epsilon = 1e-05
bf16 = jnp.bfloat16
f32 = jnp.float32
nt_dims = (((1,), (1,)), ((), ()))
tn_dims = (((0,), (0,)), ((), ()))
ANY = pl.BlockSpec(memory_space=pl.ANY)
VMEM = pl.BlockSpec(memory_space=pltpu.VMEM)
SMEM = pl.BlockSpec(memory_space=pltpu.SMEM)


def dot(a, b):
    return jnp.dot(a, b, preferred_element_type=f32)


def dot_nt(a, b):
    return lax.dot_general(a, b, nt_dims, preferred_element_type=f32)


def dot_tn(a, b):
    return lax.dot_general(a, b, tn_dims, preferred_element_type=f32)


class Sizes:
    def __init__(self, tokens, routes, w_gate):
        micro, rows, self.width = tokens.shape
        self.experts = lax.axis_size("expert")
        self.sections = lax.axis_size("section")
        self.dp = lax.axis_size("dp")
        top = routes.shape[-1]
        self.top = top
        self.hidden = w_gate.shape[-1]
        groups = micro // self.sections
        self.groups = groups
        self.tok = groups * rows
        self.cap = groups * min(rows, rows * top // self.experts + 1)
        pieces = 1
        while self.cap * pieces % 8:
            pieces *= 2
        self.pieces = pieces
        self.pw = self.width // pieces
        self.main = self.cap // 16 * 16
        self.rest = self.cap - self.main
        self.chunk = self.cap * pieces
        self.slots = self.experts * self.cap
        self.part = self.width // self.dp


def rest_mixer(z):
    per = z.experts * z.rest
    mat = np.zeros((z.pieces * per, z.experts * z.pieces * z.rest), np.float32)
    for c in range(z.experts):
        for p in range(z.pieces):
            for r in range(z.rest):
                mat[p * per + c * z.rest + r, c * z.pieces * z.rest + p * z.rest + r] = 1
    return jnp.asarray(mat, bf16)


def to_pieces(z, value):
    return jnp.concatenate([value[:, p * z.pw : (p + 1) * z.pw] for p in range(z.pieces)], 0)


def sum_pieces(z, column):
    total = column[: z.tok]
    for p in range(1, z.pieces):
        total = total + column[p * z.tok : (p + 1) * z.tok]
    return jnp.concatenate([total] * z.pieces, 0)


def gather_rows(z, chunks, mixer, dst):
    for c in range(z.experts):
        for p in range(z.pieces):
            if z.main:
                dst[c * z.main : (c + 1) * z.main, p * z.pw : (p + 1) * z.pw] = chunks[c][
                    p * z.main : (p + 1) * z.main, :
                ]
    base = z.experts * z.main
    per = z.experts * z.rest
    if z.rest:
        tail = jnp.concatenate([chunks[c][z.pieces * z.main :, :] for c in range(z.experts)], 0)
        mixed = dot(mixer[...], tail).astype(bf16)
        for p in range(z.pieces):
            dst[base : base + per, p * z.pw : (p + 1) * z.pw] = mixed[p * per : (p + 1) * per]


def scatter_rows(z, value, mixer, chunks):
    for c in range(z.experts):
        for p in range(z.pieces):
            if z.main:
                chunks[c][p * z.main : (p + 1) * z.main, :] = value[
                    c * z.main : (c + 1) * z.main, p * z.pw : (p + 1) * z.pw
                ]
    base = z.experts * z.main
    per = z.pieces * z.rest
    if z.rest:
        tail = to_pieces(z, value[base:])
        mixed = dot_tn(mixer[...], tail).astype(bf16)
        for c in range(z.experts):
            chunks[c][z.pieces * z.main :, :] = mixed[c * per : (c + 1) * per]


def selector(z, row):
    number = lax.broadcasted_iota(jnp.int32, (z.experts * z.chunk, z.pieces * z.tok), 0)
    return (number.astype(f32) == row).astype(bf16)


def selector_t(z, column):
    number = lax.broadcasted_iota(jnp.int32, (z.pieces * z.tok, z.experts * z.chunk), 1)
    return (number.astype(f32) == column).astype(bf16)


def write_chunks(z, value, outs):
    for c in range(z.experts):
        outs[c][...] = value[c * z.chunk : (c + 1) * z.chunk]


def read_chunks(refs):
    return jnp.concatenate([r[...] for r in refs], 0)


def slot_place(z, ids, pos, piece):
    inside = pos < z.main
    base = ids * z.chunk + jnp.where(inside, pos, z.pieces * z.main + pos - z.main)
    return base + piece * jnp.where(inside, float(z.main), float(z.rest))


def half_rows(z, sec, ref):
    start = sec[0] * z.groups
    return jnp.concatenate([ref[start + g] for g in range(z.groups)], 0)


def start_kernel(z, sec, routes_a, routes_b, probs_a, probs_b, tokens, rowtab, coltab, *outs):
    first = sec[0] == 0
    me = sec[2]

    def columns(ref, mix):
        rows = ref.shape[-1]
        diagonal = lax.broadcasted_iota(jnp.int32, (rows, rows), 0) == lax.broadcasted_iota(
            jnp.int32, (rows, rows), 1
        )
        found = []
        for k in range(z.top):
            pieces = []
            for g in range(z.groups):
                line = mix(ref[sec[0] * z.groups + g][k : k + 1, :])
                pieces.append(jnp.sum(jnp.where(diagonal, line, 0.0), 1, keepdims=True))
            found.append(jnp.concatenate(pieces, 0))
        return found

    number = lambda v: (v ^ me).astype(f32)
    ids_a, ids_b = columns(routes_a, number), columns(routes_b, number)
    weight_a, weight_b = columns(probs_a, lambda v: v), columns(probs_b, lambda v: v)
    pick = lambda a, b: [jnp.where(first, p, q) for p, q in zip(a, b)]
    layers = (pick(ids_a, ids_b), pick(ids_b, ids_a))
    weights = (pick(weight_a, weight_b), pick(weight_b, weight_a))
    wide = z.pieces * z.tok
    row_t = lax.broadcasted_iota(jnp.int32, (z.tok, wide), 0)
    lane = lax.broadcasted_iota(jnp.int32, (1, wide), 1)
    lane_p = jnp.zeros((1, wide), jnp.int32)
    for p in range(1, z.pieces):
        lane_p = lane_p + (lane >= p * z.tok).astype(jnp.int32)
    lane_t = lane - lane_p * z.tok
    same = row_t == lane_t
    before = row_t < lane_t
    col_t = lax.broadcasted_iota(jnp.int32, (z.tok, z.tok), 0)
    col_u = lax.broadcasted_iota(jnp.int32, (z.tok, z.tok), 1)
    narrow_same = col_t == col_u
    narrow_before = col_u < col_t
    row_list = []
    col_list = []
    for layer in layers:
        cols = layer
        rows = [jnp.sum(jnp.where(same, c, 0.0), 0, keepdims=True) for c in cols]
        thin = [jnp.sum(jnp.where(narrow_same, c, 0.0), 0, keepdims=True) for c in cols]
        for k in range(z.top):
            count = sum((c == rows[k]).astype(f32) for c in cols)
            pos = jnp.sum(jnp.where(before, count, 0.0), 0, keepdims=True)
            row_list.append(slot_place(z, rows[k], pos, lane_p.astype(f32)))
            count = sum((cols[k] == r).astype(f32) for r in thin)
            pos = jnp.sum(jnp.where(narrow_before, count, 0.0), 1, keepdims=True)
            col_list.append(
                jnp.concatenate(
                    [slot_place(z, cols[k], pos, float(p)) for p in range(z.pieces)], 0
                )
            )
    for weight in weights:
        for k in range(z.top):
            col_list.append(jnp.concatenate([weight[k]] * z.pieces, 0))
    lanes = lax.broadcasted_iota(jnp.int32, coltab.shape, 1)
    packed = jnp.zeros(coltab.shape, f32)
    for j, col in enumerate(col_list):
        packed = jnp.where(lanes == j, col, packed)
    coltab[...] = packed
    for j, row in enumerate(row_list):
        rowtab[j : j + 1, :] = row
    x = half_rows(z, sec, tokens).astype(f32)
    inv = lax.rsqrt(jnp.mean(x * x, -1, keepdims=True) + epsilon)
    normed = to_pieces(z, (x * inv).astype(bf16))
    select = sum(selector(z, row_list[k]) for k in range(z.top))
    write_chunks(z, dot(select, normed).astype(bf16), outs)


def scaled_dispatch(z, upstream, rowtab, coltab, layer):
    total = 0.0
    probs = z.sections * z.top
    for k in range(z.top):
        at = layer * z.top + k
        scaled = (coltab[:, probs + at : probs + at + 1] * upstream).astype(bf16)
        total = total + dot(selector(z, rowtab[at : at + 1, :]), scaled)
    return total.astype(bf16)


def load_start(sec, layer, own, far, dst, sem):
    mine = sec[0] == layer
    pl.when(mine)(lambda: pltpu.make_async_copy(own, dst, sem).start())
    pl.when(jnp.logical_not(mine))(lambda: pltpu.make_async_copy(far, dst, sem).start())


def load_wait(own, dst, sem):
    pltpu.make_async_copy(own, dst, sem).wait()


def cotangent_kernel(z, sec, rowtab, coltab, cot, mixer, *refs):
    own, far = refs[:3], refs[3:6]
    even, odd, mixer_out, *held, sems = refs[6:]
    for i in range(3):
        load_start(sec, 0, own[i], far[i], held[i], sems.at[i])
    mixer_out[...] = mixer[...]
    upstream = to_pieces(z, half_rows(z, sec, cot)).astype(f32)
    sent = scaled_dispatch(z, upstream, rowtab, coltab, 1)
    for c in range(z.experts):
        at = c // 2 * z.chunk
        (odd if c % 2 else even)[at : at + z.chunk, :] = sent[c * z.chunk : (c + 1) * z.chunk]
    for i in range(3):
        load_wait(own[i], held[i], sems.at[i])


def relay_kernel(z, even, odd, *outs):
    for j, out in enumerate(outs):
        at = j * z.chunk
        out[: z.chunk, :] = even[at : at + z.chunk, :]
        out[z.chunk :, :] = odd[at : at + z.chunk, :]


def write_parts(z, dp_pos, src, outs):
    for m in range(z.dp):

        @pl.when(dp_pos == m)
        def _():
            for k in range(z.dp):
                at = (m ^ k) * z.part
                outs[k][...] = src[:, at : at + z.part]


def forward_kernel(z, sec, mixer, vg, vu, vd, *refs):
    recv, refs = refs[: z.experts], refs[z.experts :]
    outs, refs = refs[: z.experts], refs[z.experts :]
    parts = refs[: z.dp]
    gate_out, up_out, both_out, rows = refs[z.dp :]
    gather_rows(z, recv, mixer, rows)
    gate = dot(rows[...], vg[...])
    up = dot(rows[...], vu[...])
    act = (gate * jax.nn.sigmoid(gate) * up).astype(bf16)
    scatter_rows(z, dot(act, vd[...]).astype(bf16), mixer, outs)
    gate_out[...] = gate
    up_out[...] = up
    both_out[:, : z.hidden] = gate.astype(bf16)
    both_out[:, z.hidden :] = up.astype(bf16)
    write_parts(z, sec[1], rows, parts)


def middle_kernel(z, sec, rowtab, coltab, tokens, *refs):
    recv = refs[: z.experts]
    kept = refs[z.experts]
    outs = refs[z.experts + 1 :]
    back = read_chunks(recv)
    probs = z.sections * z.top
    mixed = 0.0
    for k in range(z.top):
        chosen = dot(selector_t(z, coltab[:, k : k + 1]), back)
        mixed = mixed + coltab[:, probs + k : probs + k + 1] * chosen
    x = (to_pieces(z, half_rows(z, sec, tokens)).astype(f32) + mixed).astype(bf16)
    kept[...] = x
    xf = x.astype(f32)
    square = sum_pieces(z, jnp.sum(xf * xf, -1, keepdims=True))
    normed = (xf * lax.rsqrt(square / z.width + epsilon)).astype(bf16)
    select = sum(selector(z, rowtab[z.top + k : z.top + k + 1, :]) for k in range(z.top))
    write_chunks(z, dot(select, normed).astype(bf16), outs)


def hidden_grads(gate, up, back):
    sg = jax.nn.sigmoid(gate)
    silu = gate * sg
    d_gate = (back * up * sg * (1.0 + gate * (1.0 - sg))).astype(bf16)
    d_up = (back * silu).astype(bf16)
    return d_gate, d_up, (silu * up).astype(bf16)


def given_kernel(z, sec, mixer, *refs):
    half = z.experts // 2
    pairs, own, far, refs = refs[:half], refs[half : half + 3], refs[half + 3 : half + 6], refs[half + 6 :]
    parts, refs = refs[: z.dp], refs[z.dp :]
    back_out, vg, vu, go, vd, sems = refs
    held = (vg, vu, vd)
    for i in (2, 0, 1):
        load_start(sec, 1, own[i], far[i], held[i], sems.at[i])
    chunks = [pairs[c // 2].at[pl.ds(c % 2 * z.chunk, z.chunk)] for c in range(z.experts)]
    gather_rows(z, chunks, mixer, go)
    write_parts(z, sec[1], go, parts)
    load_wait(own[2], vd, sems.at[2])
    back_out[...] = dot_nt(go[...], vd[...])
    for i in range(2):
        load_wait(own[i], held[i], sems.at[i])


def turn_kernel(z, sec, mixer, vg, vu, back, *refs):
    recv, refs = refs[: z.experts], refs[z.experts :]
    outs, refs = refs[: z.experts], refs[z.experts :]
    row_parts = refs[: z.dp]
    act_out, dgu_out, rows = refs[z.dp :]
    gather_rows(z, recv, mixer, rows)
    gate = dot(rows[...], vg[...])
    up = dot(rows[...], vu[...])
    d_gate, d_up, act = hidden_grads(gate, up, back[...])
    act_out[...] = act
    dgu_out[:, : z.hidden] = d_gate
    dgu_out[:, z.hidden :] = d_up
    d_rows = (dot_nt(d_gate, vg[...]) + dot_nt(d_up, vu[...])).astype(bf16)
    scatter_rows(z, d_rows, mixer, outs)
    write_parts(z, sec[1], rows, row_parts)


def upstream_kernel(z, sec, rowtab, coltab, kept, cot, *refs):
    recv = refs[: z.experts]
    outs = refs[z.experts :]
    back = read_chunks(recv)
    select = sum(
        selector_t(z, coltab[:, z.top + k : z.top + k + 1]) for k in range(z.top)
    )
    d_normed = dot(select, back)
    xf = kept[...].astype(f32)
    square = sum_pieces(z, jnp.sum(xf * xf, -1, keepdims=True))
    inv = lax.rsqrt(square / z.width + epsilon)
    inner = sum_pieces(z, jnp.sum(d_normed * xf, -1, keepdims=True)) / z.width
    d_x = inv * d_normed - xf * (inv * inv * inv) * inner
    upstream = (to_pieces(z, half_rows(z, sec, cot)).astype(f32) + d_x).astype(bf16).astype(f32)
    write_chunks(z, scaled_dispatch(z, upstream, rowtab, coltab, 0), outs)


def pre_values(z, gate, up, boths, g):
    if g == 0:
        return gate[...], up[...]
    value = boths[g - 1][...].astype(f32)
    return value[:, : z.hidden], value[:, z.hidden :]


def pack_kernel(z, sec, gate, up, *refs):
    n = z.dp
    boths, refs = refs[: n - 1], refs[n - 1 :]
    rows0, rows1, acts, gos, dgus = [refs[i * n : (i + 1) * n] for i in range(5)]
    keep_rows, keep_act, send_rows, send_act, keep_go, keep_dgu = refs[5 * n :]
    first = sec[0] == 0
    for g in range(n):
        at = pl.ds(g * z.slots, z.slots)
        pre_gate, pre_up = pre_values(z, gate, up, boths, g)
        act0 = (pre_gate * jax.nn.sigmoid(pre_gate) * pre_up).astype(bf16)

        @pl.when(first)
        def _():
            keep_rows[at, :] = rows0[g][...]
            keep_act[at, :] = act0
            send_rows[at, :] = rows1[g][...]
            send_act[at, :] = acts[g][...]

        @pl.when(jnp.logical_not(first))
        def _():
            keep_rows[at, :] = rows1[g][...]
            keep_act[at, :] = acts[g][...]
            send_rows[at, :] = rows0[g][...]
            send_act[at, :] = act0

        keep_go[at, :] = gos[g][...]
        keep_dgu[at, :] = dgus[g][...]


def stack_kernel(z, *refs):
    out = refs[-1]
    for c, ref in enumerate(refs[:-1]):
        out[c * z.chunk : (c + 1) * z.chunk, :] = ref[...]


def turned_kernel(z, rows_a, rows_b, act_a, act_b, rows_t, act_t):
    rows_t[...] = jnp.concatenate([rows_a[...], rows_b[...]], 0).T
    act_t[...] = jnp.concatenate([act_a[...], act_b[...]], 0).T


def backward_kernel(z, sec, mixer, vd, gate, up, *refs):
    ne, n, early = z.experts, z.dp, z.experts // 2
    boths, refs = refs[: n - 1], refs[n - 1 :]
    recv, refs = refs[:ne], refs[ne:]
    go_out, dgu_out, go = refs[-3:]
    for g in range(n):
        if g:
            stacked, refs = refs[0], refs[1:]
            late, refs = refs[: ne - early], refs[ne - early :]
            recv = [stacked.at[pl.ds(c * z.chunk, z.chunk)] for c in range(early)]
            recv = recv + list(late)
        gather_rows(z, recv, mixer, go.at[pl.ds(g * z.slots, z.slots)])

    back = dot_nt(go[...], vd[...])
    for g in range(n):
        at = slice(g * z.slots, (g + 1) * z.slots)
        pre_gate, pre_up = pre_values(z, gate, up, boths, g)
        d_gate, d_up, _ = hidden_grads(pre_gate, pre_up, back[at])
        dgu_out[at, : z.hidden] = d_gate
        dgu_out[at, z.hidden :] = d_up
    for m in range(n):

        @pl.when(sec[1] == m)
        def _():
            go_out[...] = go[:, m * z.part : (m + 1) * z.part]


def grads_kernel(z, sec, rows_t, act_t, goes, dgus, *refs):
    far_goes, far_dgus, own_go, own_dgu, far_go, far_dgu = refs[:6]
    out_gate, out_up, out_down, go, dgu, buf_gate, buf_up, buf_down, sems = refs[6:]
    per = z.dp * z.slots
    first = sec[0] == 0

    @pl.when(first)
    def _():
        dgu[:per, :] = own_dgu[...]
        dgu[per:, :] = far_dgu[...]
        go[:per, :] = own_go[...]
        go[per:, :] = far_go[...]

    @pl.when(jnp.logical_not(first))
    def _():
        dgu[:per, :] = dgus[...]
        dgu[per:, :] = far_dgus[...]
        go[:per, :] = goes[...]
        go[per:, :] = far_goes[...]

    copies = []

    def send(src, dst, at, size):
        copy = pltpu.make_async_copy(
            src.at[pl.ds(at, size)], dst.at[pl.ds(at, size)], sems.at[len(copies)]
        )
        copy.start()
        copies.append(copy)

    step = z.part // 4
    for at in range(0, z.part, step):
        block = dot(rows_t[at : at + step, :], dgu[...])
        buf_gate[at : at + step, :] = block[:, : z.hidden]
        send(buf_gate, out_gate, at, step)
        buf_up[at : at + step, :] = block[:, z.hidden :]
        send(buf_up, out_up, at, step)
    step = z.hidden // 5
    for at in range(0, z.hidden, step):
        buf_down[at : at + step, :] = dot(act_t[at : at + step, :], go[...])
        send(buf_down, out_down, at, step)
    for copy in copies:
        copy.wait()


class Far:
    def __init__(self, value):
        self.value = value


class Near(Far):
    pass


def exchange(axis, parts):
    size = lax.axis_size(axis)
    out = [parts[0]]
    for k in range(1, size):
        out.append(lax.ppermute(parts[k], axis, [(i, i ^ k) for i in range(size)]))
    return out


def shards(tokens, routes, gate_probs, w_gate, w_up, w_down, cotangent):
    z = Sizes(tokens, routes, w_gate)
    ne, n = z.experts, z.dp
    positions = [lax.axis_index(a) for a in ("section", "dp", "expert")]
    sec = jnp.stack(positions).astype(jnp.int32)

    def swap(value):
        return exchange("section", [value, value])[1]

    def gather_dp(value):
        return exchange("dp", [value] * n)

    def call(body, values, outs, scratch=(), limit=24):
        specs, fixed = [SMEM], []
        for v in values:
            specs.append(ANY if type(v) is Far else VMEM)
            if isinstance(v, Far):
                fixed.append(v.value)
            else:
                fixed.append(pltpu.with_memory_space_constraint(v, pltpu.VMEM))
        return pl.pallas_call(
            lambda *refs: body(z, *refs),
            in_specs=specs,
            out_shape=outs,
            out_specs=[ANY if isinstance(o, jax.ShapeDtypeStruct) else VMEM for o in outs],
            scratch_shapes=list(scratch),
            compiler_params=pltpu.CompilerParams(vmem_limit_bytes=limit << 20),
        )(sec, *fixed)

    vm = lambda *s: pltpu.VMEM(s, bf16)
    fl = lambda *s: pltpu.VMEM(s, f32)
    wide = z.pieces * z.tok
    chunks = [vm(z.chunk, z.pw)] * ne
    parts = [vm(z.slots, z.part)] * n
    per = n * z.slots
    no_sec = lambda body: lambda z, sec, *refs: body(z, *refs)

    lined_routes = jnp.swapaxes(routes[0], 1, 2)
    lined_probs = jnp.swapaxes(gate_probs[0], 1, 2)
    far_routes, far_probs = swap(lined_routes), swap(lined_probs)
    own = [w_gate[0, 0], w_up[0, 0], w_down[0, 0]]
    far = [swap(w) for w in own]
    every = [Far(w) for w in own + far]
    held = [vm(z.width, z.hidden), vm(z.width, z.hidden), vm(z.hidden, z.width)]
    load_sems = pltpu.SemaphoreType.DMA((3,))

    rowtab, coltab, *send = call(
        start_kernel,
        [Near(lined_routes), far_routes, Near(lined_probs), far_probs, Near(tokens)],
        [fl(8, wide), fl(wide, 8)] + chunks,
    )
    recv = exchange("expert", send)
    half = ne // 2
    stack = vm(half * z.chunk, z.pw)
    even, odd, mixer, *held0 = call(
        cotangent_kernel,
        [rowtab, coltab, cotangent, Near(rest_mixer(z))] + every,
        [stack, stack, vm(*rest_mixer(z).shape)] + held,
        [load_sems],
    )

    def xor(value, k):
        return lax.ppermute(value, "expert", [(i, i ^ k) for i in range(ne)])

    pair = vm(2 * z.chunk, z.pw)
    pairs = call(no_sec(relay_kernel), [even, xor(odd, 1)], [pair] * half)
    given = [pairs[0]] + [xor(pairs[j], 2 * j) for j in range(1, half)]
    out = call(
        forward_kernel,
        [mixer, *held0, *recv],
        chunks + parts + [fl(z.slots, z.hidden)] * 2 + [vm(z.slots, 2 * z.hidden)],
        [vm(z.slots, z.width)],
    )
    send, parts0, (gate0, up0, both0) = out[:ne], out[ne : ne + n], out[ne + n :]
    recv = exchange("expert", send)
    rows0 = exchange("dp", parts0)
    boths = gather_dp(both0)[1:]
    kept, *send = call(middle_kernel, [rowtab, coltab, tokens, *recv], [vm(wide, z.pw)] + chunks)
    recv = exchange("expert", send)
    *go_parts, back1, vg1, vu1 = call(
        given_kernel,
        [mixer, *given] + every,
        parts + [fl(z.slots, z.hidden)] + held[:2],
        [vm(z.slots, z.width), held[2], load_sems],
    )
    gos = exchange("dp", go_parts)
    out = call(
        turn_kernel,
        [mixer, vg1, vu1, back1, *recv],
        chunks + parts + [vm(z.slots, z.hidden), vm(z.slots, 2 * z.hidden)],
        [vm(z.slots, z.width)],
    )
    send, parts1, (act1, dgu1) = out[:ne], out[ne : ne + n], out[ne + n :]
    recv = exchange("expert", send)
    dgus = gather_dp(dgu1)
    rows1 = exchange("dp", parts1)
    acts = gather_dp(act1)
    send = call(upstream_kernel, [rowtab, coltab, kept, cotangent, *recv], chunks)
    recv = exchange("expert", send)
    early = ne // 2
    stacked = call(no_sec(stack_kernel), recv[:early], [vm(early * z.chunk, z.pw)])[0]
    stacked = gather_dp(stacked)[1:]
    late = [gather_dp(recv[c])[1:] for c in range(early, ne)]
    others = [v for g in range(n - 1) for v in [stacked[g]] + [l[g] for l in late]]
    keep_rows, keep_act, send_rows, send_act, keep_go, keep_dgu = call(
        pack_kernel,
        [gate0, up0, *boths, *rows0, *rows1, *acts, *gos, *dgus],
        [vm(per, z.part), vm(per, z.hidden)] * 2 + [vm(per, z.part), vm(per, 2 * z.hidden)],
    )
    far_go1, far_dgu1 = swap(keep_go), swap(keep_dgu)
    rows_t, act_t = call(
        no_sec(turned_kernel),
        [keep_rows, swap(send_rows), keep_act, swap(send_act)],
        [vm(z.part, 2 * per), vm(z.hidden, 2 * per)],
    )
    go0, dgu0 = call(
        backward_kernel,
        [mixer, held0[2], gate0, up0, *boths, *recv, *others],
        [vm(per, z.part), vm(per, 2 * z.hidden)],
        [vm(per, z.width)],
    )
    grad_shapes = [
        jax.ShapeDtypeStruct((z.part, z.hidden), f32),
        jax.ShapeDtypeStruct((z.part, z.hidden), f32),
        jax.ShapeDtypeStruct((z.hidden, z.part), f32),
    ]
    grads = call(
        grads_kernel,
        [rows_t, act_t, keep_go, keep_dgu, far_go1, far_dgu1]
        + [go0, dgu0, swap(go0), swap(dgu0)],
        grad_shapes,
        [vm(2 * per, z.part), vm(2 * per, 2 * z.hidden)]
        + [fl(*s.shape) for s in grad_shapes]
        + [pltpu.SemaphoreType.DMA((13,))],
    )
    return tuple(g[None, None] for g in grads)


def solution(mesh):
    in_specs = (
        P(None, ("expert", "dp"), None),
        P("section", None, ("expert", "dp"), None),
        P("section", None, ("expert", "dp"), None),
        P("section", "expert", None, None),
        P("section", "expert", None, None),
        P("section", "expert", None, None),
        P(None, ("expert", "dp"), None),
    )
    out_specs = (
        P("section", "expert", "dp", None),
        P("section", "expert", "dp", None),
        P("section", "expert", None, "dp"),
    )

    return jax.shard_map(shards, mesh=mesh, in_specs=in_specs, out_specs=out_specs, check_vma=False)
```
